256 devices in a mesh: expert: 64 (over x, z, core), dp: 4 (over y).
Axes of the slice: x: 4, y: 4, z: 8, core: 2. Of those that a mesh axis runs over, the one named last changes fastest.
Arguments:
- tokens: bfloat16 [8192, 3584], P('expert', 'dp'), may hold values from -6 to 6
- cotangent: bfloat16 [8192, 3584], P('expert', 'dp'), may hold values from -6 to 6
- expert_ids: int32 [8192, 8], P('expert'), may hold values from 0 to 63, all different within a row; in each aligned block of 128 rows (0 to 127, 128 to 255, ...) at most 18 rows name the same one
- gate_units: int32 [8192, 8], P('expert'), may hold values from 1 to 255
- w_in: bfloat16 [64, 3584, 1024], P('expert', 'dp'), may hold values from -0.09375 to 0.09375
- w_out: bfloat16 [64, 1024, 3584], P('expert', None, 'dp'), may hold values from -0.1875 to 0.1875
- shared_in: bfloat16 [3584, 1024], P('dp', 'expert'), may hold values from -0.09375 to 0.09375
- shared_out: bfloat16 [1024, 3584], P('expert', 'dp'), may hold values from -0.1875 to 0.1875
Outputs:
- mixed_out: bfloat16 [8192, 3584], P('expert', 'dp')
- input_grad: bfloat16 [8192, 3584], P('expert', 'dp')
- grad_w_in: bfloat16 [64, 3584, 1024], P('expert', 'dp')
- grad_w_out: bfloat16 [64, 1024, 3584], P('expert', None, 'dp')
- grad_shared_in: bfloat16 [3584, 1024], P('dp', 'expert')
- grad_shared_out: bfloat16 [1024, 3584], P('expert', 'dp')
The draws below stay inside these ranges and needn't reach their ends.
Inputs may be any that keep to these rules, and one draw needn't show every extreme that they name: `expert_ids`: each row names 8 different experts. In each aligned block of 128 rows (the tokens of one index of expert) no expert is named by more than 18 rows, a bound that some block reaches.
All inputs are finite; a program needn't handle non-finite values.
Results may differ from the reference program's by a relative error of at most 0.02.
Values may be sent and summed in bfloat16 or wider, within the bound.
No kernel may reach another device: no remote copies, remote signals or barrier semaphores. Data moves between devices by JAX's collectives and lax.ppermute only.
A program may use at most 128 MiB of HBM per device.

```python
import math
import jax
import jax.numpy as jnp
import numpy as np
from jax import lax

D = 3584
FF = 1024
SF = 1024
TOPK = 8
TOK = 128
NEXP = 64
CAP = 18
TOKENS = 8192
N_DP = 4


def place_ends(drawn, own_key, low, top_value):
    longest = drawn.shape.index(max(drawn.shape))
    spots = []
    for shift in (0, 1):
        where = [jax.random.randint(jax.random.fold_in(own_key, axis), (), 0, length) for axis, length in enumerate(drawn.shape)]
        where[longest] = (where[longest] + shift) % drawn.shape[longest]
        spots.append(tuple(where))
    return drawn.at[spots[0]].set(low).at[spots[1]].set(top_value)


def level_of(key, extent, shards, low, high):
    gain, own = 1.0, jax.random.fold_in(key, 6)
    for position, parts in shards:
        heights = jnp.exp(jax.random.uniform(jax.random.fold_in(own, position), (parts,), jnp.float32, low / len(shards), high / len(shards)))
        gain = gain * jnp.repeat(heights, extent[position] // parts).reshape([-1 if axis == position else 1 for axis in range(len(extent))])
    return gain


def assign_block(own_key, own, number, rows, count, top, reach, skew):
    sequence = jax.random.permutation(own_key, count)
    crowded, ordinary = load_shares(count, rows * top, reach, skew, True), load_shares(count, rows * top, reach, skew, False)
    places = jnp.arange(count)

    def named(sizes, offset_by):
        used = int((sizes > 0).sum())
        fixed = max(1, used // 4)
        moved = fixed + (places - fixed + offset_by * (used - fixed)) % max(1, count - fixed)
        return jnp.zeros((count,), jnp.int32).at[sequence[jnp.where(places < fixed, places, moved)]].set(jnp.asarray(sizes, jnp.int32))

    sizes = jnp.where(number % 4 == 0, named(crowded, number // 4), named(ordinary, number - number // 4 - 1))
    mixed = jax.random.permutation(jax.random.fold_in(own, 3), count)
    giver, receiver = mixed[0:count // 2 * 2:2], mixed[1:count // 2 * 2:2]
    room = jnp.minimum(sizes[giver] - 1, reach - sizes[receiver]) // 2
    room = jnp.where((giver == sequence[0]) | (receiver == sequence[0]) | (sizes[receiver] == 0), 0, jnp.maximum(room, 0))
    moved = jax.random.randint(jax.random.fold_in(own, 4), (count // 2,), 0, 1 << 20) % (room + 1)
    sizes = sizes.at[giver].add(-moved).at[receiver].add(moved)
    members = jnp.searchsorted(jnp.cumsum(sizes), jnp.arange(rows * top), side="right").astype(jnp.int32)
    listing = members.reshape(top, rows).T
    listing = listing[jax.random.permutation(jax.random.fold_in(own, 1), rows)]
    offset_by = jax.random.randint(jax.random.fold_in(own, 2), (rows, 1), 0, top)
    return jnp.take_along_axis(listing, (jnp.arange(top)[None, :] + offset_by) % top, axis=1)


def load_shares(amount, total, limit, slope, full):
    weights = [(1 << 20) // math.isqrt(standing ** slope) + 1 for standing in range(1, amount + 1)]
    largest = limit if full else min(limit, max(-(-total // amount), total * weights[0] // sum(weights)))
    least = 1 if total - largest >= amount - 1 else 0
    counts, rest = [largest] + [least] * (amount - 1), total - largest - least * (amount - 1)
    while rest > 0:
        free = [i for i in range(1, amount) if counts[i] < largest] or [i for i in range(1, amount) if counts[i] < limit]
        whole, budget = sum([weights[i] for i in free]), rest
        for i in free:
            more = min(limit - counts[i], max(1, budget * weights[i] // whole), rest)
            counts[i] = counts[i] + more
            rest = rest - more
    return np.array(counts)


def centred(rng, extent, deviation, limit, cuts=(), kind=jnp.bfloat16):
    factor_of = level_of(rng, extent, cuts, -0.22, 0.18) if cuts else 1.0
    entries = jax.random.normal(rng, extent, jnp.float32) * deviation * factor_of
    return jnp.minimum(jnp.maximum(entries, -limit), limit).astype(kind)


def setup_inputs(seed: int = 0) -> dict:
    key_of = jax.random.split(jax.random.key(seed), 9)
    tokens = centred(key_of[0], (TOKENS, D), 1.0, 6.0, ((0, 64), (1, 4)))
    cotangent = centred(key_of[1], (TOKENS, D), 1.0, 6.0, ((0, 64), (1, 4)))
    expert_ids_keys = jax.random.split(jax.random.fold_in(key_of[2], 1), TOKENS // TOK)
    expert_ids_turns = jax.random.permutation(jax.random.fold_in(key_of[2], 3), TOKENS // TOK)
    expert_ids = jax.vmap(lambda own, number: assign_block(jax.random.fold_in(key_of[2], 2), own, number, TOK, NEXP, TOPK, CAP, 2))(expert_ids_keys, expert_ids_turns).reshape((TOKENS, TOPK))
    gate_units = place_ends(jax.random.randint(key_of[3], (TOKENS, TOPK), 1, 256), jax.random.fold_in(key_of[3], 1), 1, 255).astype(jnp.int32)
    w_in = centred(key_of[4], (NEXP, D, FF), D ** -0.5, 0.09375, ((0, 64), (1, 4)))
    w_out = centred(key_of[5], (NEXP, FF, D), FF ** -0.5, 0.1875, ((0, 64), (2, 4)))
    shared_in = centred(key_of[6], (D, SF), D ** -0.5, 0.09375, ((0, 4), (1, 64)))
    shared_out = centred(key_of[7], (SF, D), SF ** -0.5, 0.1875, ((0, 64), (1, 4)))
    return {"tokens": tokens, "cotangent": cotangent, "expert_ids": expert_ids, "gate_units": gate_units, "w_in": w_in, "w_out": w_out, "shared_in": shared_in, "shared_out": shared_out}


def silu_slope(inputs):
    logistic = jax.nn.sigmoid(inputs)
    return logistic * (1.0 + inputs * (1.0 - logistic))


def contract(first_op, second_op, first_axis, second_axis):
    return lax.dot_general(first_op, second_op, (((first_axis,), (second_axis,)), ((), ())), preferred_element_type=jnp.float32)


def block_sum(first_op, second_op, second_axis):
    block_width = first_op.shape[1] // N_DP
    summed = jnp.zeros((first_op.shape[0], second_op.shape[1 - second_axis]), jnp.float32)
    for block_id in range(N_DP):
        first_part = lax.slice_in_dim(first_op, block_id * block_width, (block_id + 1) * block_width, axis=1)
        second_part = lax.slice_in_dim(second_op, block_id * block_width, (block_id + 1) * block_width, axis=second_axis)
        partial_value = contract(first_part, second_part, 1, second_axis)
        summed = summed + lax.optimization_barrier(partial_value.astype(jnp.bfloat16)).astype(jnp.float32)
    return summed


def reference(tokens, cotangent, expert_ids, gate_units, w_in, w_out, shared_in, shared_out):
    pair_count = TOKENS * TOPK
    most_rows = NEXP * CAP
    flat_ids = expert_ids.reshape(pair_count)
    weights = gate_units.reshape(pair_count).astype(jnp.float32) / 256.0
    shared_pre = block_sum(tokens, shared_in, 0)
    shared_hidden = jax.nn.silu(shared_pre).astype(jnp.bfloat16)
    shared_y = jnp.dot(shared_hidden, shared_out, preferred_element_type=jnp.float32)
    shared_hgrad = block_sum(cotangent, shared_out, 1)
    shared_pgrad = (shared_hgrad * silu_slope(shared_pre)).astype(jnp.bfloat16)
    shared_dx = contract(shared_pgrad, shared_in, 1, 1)
    grad_shared_in = contract(tokens, shared_pgrad, 0, 0).astype(jnp.bfloat16)
    grad_shared_out = contract(shared_hidden, cotangent, 0, 0).astype(jnp.bfloat16)

    def one_expert(running, expert_index):
        routed_y, routed_dx = running
        chosen = jnp.nonzero(flat_ids == expert_index, size=most_rows, fill_value=pair_count)[0].astype(jnp.int32)
        is_live = chosen < pair_count
        bounded = jnp.minimum(chosen, pair_count - 1).astype(jnp.int32)
        token_index = (bounded // TOPK).astype(jnp.int32)
        weighting = jnp.where(is_live, weights[bounded], jnp.float32(0.0))
        rows_in = jnp.where(is_live[:, None], tokens[token_index], jnp.zeros((), jnp.bfloat16)).astype(jnp.bfloat16)
        pre_act = block_sum(rows_in, w_in[expert_index], 0)
        hidden = jax.nn.silu(pre_act).astype(jnp.bfloat16)
        out_rows = jnp.dot(hidden, w_out[expert_index], preferred_element_type=jnp.float32).astype(jnp.bfloat16)
        grad_rows = (weighting[:, None] * cotangent[token_index].astype(jnp.float32)).astype(jnp.bfloat16)
        hidden_grad = block_sum(grad_rows, w_out[expert_index], 1)
        pre_grad = (hidden_grad * silu_slope(pre_act)).astype(jnp.bfloat16)
        dx_rows = contract(pre_grad, w_in[expert_index], 1, 1).astype(jnp.bfloat16)
        target = jnp.where(is_live, token_index, jnp.int32(TOKENS)).astype(jnp.int32)
        routed_y = routed_y.at[target].add(weighting[:, None] * out_rows.astype(jnp.float32), mode="drop")
        routed_dx = routed_dx.at[target].add(dx_rows.astype(jnp.float32), mode="drop")
        g_in = contract(rows_in, pre_grad, 0, 0).astype(jnp.bfloat16)
        g_out = contract(hidden, grad_rows, 0, 0).astype(jnp.bfloat16)
        return (routed_y, routed_dx), (g_in, g_out)

    start = (jnp.zeros((TOKENS, D), jnp.float32), jnp.zeros((TOKENS, D), jnp.float32))
    (routed_y, routed_dx), (grad_w_in, grad_w_out) = lax.scan(one_expert, start, jnp.arange(NEXP, dtype=jnp.int32))
    mixed_out = (shared_y + routed_y).astype(jnp.bfloat16)
    input_grad = (shared_dx + routed_dx).astype(jnp.bfloat16)
    return mixed_out, input_grad, grad_w_in, grad_w_out, grad_shared_in, grad_shared_out
```

```python
import jax
import jax.numpy as jnp
import numpy as np
from jax import lax
from jax.sharding import Mesh, PartitionSpec as P

X, Z, C, DP = 4, 8, 2, 4
PEERS = X * C
BF16, F32 = jnp.bfloat16, jnp.float32


def silu_slope(inputs):
    logistic = jax.nn.sigmoid(inputs)
    return logistic * (1.0 + inputs * (1.0 - logistic))


def contract(first_op, second_op, first_axis, second_axis):
    return lax.dot_general(
        first_op,
        second_op,
        (((first_axis,), (second_axis,)), ((), ())),
        preferred_element_type=F32,
    )


def shifted(value, axis, size, step):
    return lax.ppermute(value, axis, [(i, (i + step) % size) for i in range(size)])


def gather_ring(block):
    half = block.shape[0] // 2
    back, ahead = [block], [block]
    for _ in range(Z // 2 - 1):
        back.append(shifted(back[-1], "z", Z, 1))
        ahead.append(shifted(ahead[-1], "z", Z, -1))
    low = shifted(back[-1][:half], "z", Z, 1)
    high = shifted(ahead[-1][half:], "z", Z, -1)
    return jnp.concatenate([*ahead, low, high, *back[:0:-1]], axis=0)


def add(first, second):
    return (first.astype(F32) + second.astype(F32)).astype(BF16)


def scatter_ring(blocks):
    mid = Z // 2
    half = blocks.shape[1] // 2
    low = shifted(blocks[mid, :half], "z", Z, 1)
    high = shifted(blocks[mid, half:], "z", Z, -1)
    up = jnp.concatenate([add(blocks[mid - 1, :half], low), blocks[mid - 1, half:]], axis=0)
    down = jnp.concatenate([blocks[mid + 1, :half], add(blocks[mid + 1, half:], high)], axis=0)
    for k in range(mid - 1, 0, -1):
        up = shifted(up, "z", Z, 1)
        down = shifted(down, "z", Z, -1)
        if k > 1:
            up = add(blocks[k - 1], up)
            down = add(blocks[Z - k + 1], down)
    return (blocks[0].astype(F32) + up.astype(F32) + down.astype(F32)).astype(BF16)


def dp_scatter(part_of):
    sent = {k: shifted(part_of(k), "dp", DP, k) for k in (2, 1, 3)}
    total = part_of(0).astype(F32)
    for k in (1, 3, 2):
        total = total + sent[k].astype(F32)
    return total


def dp_gather(block, own):
    rows = block.shape[0]
    whole = jnp.zeros((DP * rows, block.shape[1]), block.dtype)
    for k in (0, 1, 3, 2):
        part = block if k == 0 else shifted(block, "dp", DP, k)
        whole = lax.dynamic_update_slice(whole, part, (((own - k) % DP) * rows, 0))
    return whole


def exchange(rows):
    return lax.all_to_all(rows, ("x", "c"), split_axis=0, concat_axis=0, tiled=True)


def local(tokens, cotangent, expert_ids, gate_units, w_in, w_out, shared_in, shared_out):
    tok_rows, features = tokens.shape
    per_token = expert_ids.shape[1]
    experts = PEERS * Z
    capacity = min(tok_rows, tok_rows * per_token // experts + tok_rows // 64)
    group = Z * capacity
    slots = PEERS * group
    line_rows = Z * tok_rows
    w_in, w_out = w_in[0], w_out[0]
    z_own, dp_own = lax.axis_index("z"), lax.axis_index("dp")

    order = np.arange(experts).reshape(X, Z, C).transpose(1, 0, 2).reshape(experts)
    named = expert_ids.T[None] == jnp.asarray(order, jnp.int32)[:, None, None]
    units = jnp.sum(jnp.where(named, gate_units.T[None], 0), axis=1)
    dense = (units.astype(F32) / 256.0).astype(BF16).reshape(Z, PEERS, tok_rows)
    dense = lax.all_to_all(dense, "z", split_axis=0, concat_axis=0, tiled=True)
    dense = lax.dynamic_slice_in_dim(jnp.concatenate([dense, dense], axis=0), z_own, Z, axis=0)
    routed = dense > 0
    before = (
        lax.broadcasted_iota(jnp.int32, (tok_rows, tok_rows), 0)
        < lax.broadcasted_iota(jnp.int32, (tok_rows, tok_rows), 1)
    ).astype(BF16)
    rank = contract(routed.astype(BF16).reshape(experts, tok_rows), before, 1, 0)
    rank = rank.reshape(Z, PEERS, tok_rows).astype(jnp.int32)
    first = (jnp.arange(Z, dtype=jnp.int32) * capacity)[:, None, None]
    slot = jnp.where(routed, rank + first, -1)
    slot = slot.transpose(1, 0, 2).reshape(PEERS, 1, line_rows)
    gates = dense.transpose(1, 0, 2).reshape(PEERS, 1, line_rows)
    taken = lax.broadcasted_iota(jnp.int32, (PEERS, group, line_rows), 1) == slot
    pick = taken.astype(BF16).reshape(slots, line_rows)
    weigh = jnp.where(taken, gates, jnp.zeros((), BF16)).reshape(slots, line_rows)

    line_tokens = gather_ring(tokens)
    line_cotangent = gather_ring(cotangent)
    own_shared = jnp.concatenate([shared_in.T, shared_out], axis=0)
    line_shared = lax.all_gather(own_shared, ("x", "c"), axis=0)
    width = shared_out.shape[0]
    line_in = line_shared[:, :width].reshape(PEERS * width, features)
    line_out = line_shared[:, width:].reshape(PEERS * width, features)

    arrived = exchange(
        contract(pick, line_tokens, 1, 0).astype(BF16).reshape(PEERS, group, features)
    ).reshape(slots, features)
    grad_rows = exchange(
        contract(weigh, line_cotangent, 1, 0).astype(BF16).reshape(PEERS, group, features)
    ).reshape(slots, features)

    shared_units = PEERS * width
    shared_part = jnp.stack(
        [
            contract(line_in, line_tokens, 1, 1).astype(BF16).reshape(DP, shared_units // DP, line_rows),
            contract(line_out, line_cotangent, 1, 1).astype(BF16).reshape(DP, shared_units // DP, line_rows),
        ],
        axis=1,
    )
    shared_sum = dp_scatter(
        lambda k: lax.dynamic_index_in_dim(shared_part, (dp_own + k) % DP, 0, keepdims=False)
    )
    shared_both = jnp.concatenate(
        [
            jax.nn.silu(shared_sum[0]).astype(BF16),
            (shared_sum[1] * silu_slope(shared_sum[0])).astype(BF16),
        ],
        axis=0,
    )
    shared_both = dp_gather(shared_both, dp_own).reshape(DP, 2, shared_units // DP, line_rows)
    shared_hidden = shared_both[:, 0].reshape(shared_units, line_rows)
    shared_pgrad = shared_both[:, 1].reshape(shared_units, line_rows)

    quarter = slots // DP

    def rows_of(value, k):
        return lax.dynamic_slice_in_dim(value, ((dp_own + k) % DP) * quarter, quarter, axis=0)

    pre_act = dp_scatter(lambda k: contract(rows_of(arrived, k), w_in, 1, 0).astype(BF16))
    hidden = dp_gather(jax.nn.silu(pre_act).astype(BF16), dp_own)
    hidden_grad = dp_scatter(lambda k: contract(rows_of(grad_rows, k), w_out, 1, 1).astype(BF16))
    pre_grad = dp_gather((hidden_grad * silu_slope(pre_act)).astype(BF16), dp_own)

    returned = exchange(
        contract(hidden, w_out, 1, 0).astype(BF16).reshape(PEERS, group, features)
    ).reshape(slots, features)
    mixed_part = contract(weigh, returned, 0, 0) + contract(shared_hidden, line_out, 0, 0)
    mixed_out = scatter_ring(mixed_part.astype(BF16).reshape(Z, tok_rows, features))

    sent_back = exchange(
        contract(pre_grad, w_in, 1, 1).astype(BF16).reshape(PEERS, group, features)
    ).reshape(slots, features)
    grad_part = contract(pick, sent_back, 0, 0) + contract(shared_pgrad, line_in, 0, 0)
    input_grad = scatter_ring(grad_part.astype(BF16).reshape(Z, tok_rows, features))

    shared_grads = jnp.concatenate(
        [
            contract(shared_pgrad, line_tokens, 1, 0).astype(BF16).reshape(PEERS, width, features),
            contract(shared_hidden, line_cotangent, 1, 0).astype(BF16).reshape(PEERS, width, features),
        ],
        axis=1,
    )
    shared_grads = jnp.sum(exchange(shared_grads).astype(F32), axis=0).astype(BF16)

    grad_w_in = contract(arrived, pre_grad, 0, 0).astype(BF16)[None]
    grad_w_out = contract(hidden, grad_rows, 0, 0).astype(BF16)[None]
    return (
        mixed_out,
        input_grad,
        grad_w_in,
        grad_w_out,
        shared_grads[:width].T,
        shared_grads[width:],
    )


def solution(mesh):
    grid = Mesh(mesh.devices.reshape(X, Z, C, DP), ("x", "z", "c", "dp"))
    expert = ("x", "z", "c")
    return jax.shard_map(
        local,
        mesh=grid,
        in_specs=(
            P(expert, "dp"),
            P(expert, "dp"),
            P(expert, None),
            P(expert, None),
            P(expert, "dp", None),
            P(expert, None, "dp"),
            P("dp", expert),
            P(expert, "dp"),
        ),
        out_specs=(
            P(expert, "dp"),
            P(expert, "dp"),
            P(expert, "dp", None),
            P(expert, None, "dp"),
            P("dp", expert),
            P(expert, "dp"),
        ),
        check_vma=False,
    )
```

```python
import jax
import jax.numpy as jnp
import numpy as np
from jax import lax
from jax.sharding import Mesh, PartitionSpec as P

X, Z, C, DP = 4, 8, 2, 4
PEERS = X * C
BF16, F32 = jnp.bfloat16, jnp.float32


def silu_slope(inputs):
    logistic = jax.nn.sigmoid(inputs)
    return logistic * (1.0 + inputs * (1.0 - logistic))


def contract(first_op, second_op, first_axis, second_axis):
    return lax.dot_general(
        first_op,
        second_op,
        (((first_axis,), (second_axis,)), ((), ())),
        preferred_element_type=F32,
    )


def shifted(value, axis, size, step):
    return lax.ppermute(value, axis, [(i, (i + step) % size) for i in range(size)])


def together(*values):
    return lax.optimization_barrier(values)


def after(value, *earlier):
    return together(value, *earlier)[0]


def gather_ring(block, axis, size, put):
    half = block.shape[0] // 2
    back = ahead = block
    rounds = []
    for k in range(1, size // 2):
        back, ahead = together(shifted(back, axis, size, 1), shifted(ahead, axis, size, -1))
        if k == 1:
            put(after(block, back), 0, 0)
        rounds.append((back, ahead))
        put(back, size - k, 0)
        put(ahead, k, 0)
    put(shifted(back[:half], axis, size, 1), size // 2, 0)
    put(shifted(ahead[half:], axis, size, -1), size // 2, half)
    return rounds


def add(first, second):
    return (first.astype(F32) + second.astype(F32)).astype(BF16)


def scatter_ring(block, axis, size, gate=None):
    mid = size // 2
    far = block(mid)
    if gate is not None:
        far = after(far, gate)
    half = far.shape[0] // 2
    low = shifted(far[:half], axis, size, 1)
    high = shifted(far[half:], axis, size, -1)
    up, down = block(mid - 1, far), block(mid + 1, far)
    up = jnp.concatenate([add(up[:half], low), up[half:]], axis=0)
    down = jnp.concatenate([down[:half], add(down[half:], high)], axis=0)
    sent = []
    for k in range(mid - 1, 0, -1):
        up, down = together(up, down)
        sent.append((up, down))
        up = shifted(up, axis, size, 1)
        down = shifted(down, axis, size, -1)
        if k > 1:
            up = add(block(k - 1), up)
            down = add(block(size - k + 1), down)
    return block(0).astype(F32) + up.astype(F32) + down.astype(F32), sent


def local(tokens, cotangent, expert_ids, gate_units, w_in, w_out, shared_in, shared_out):
    tok_rows, features = tokens.shape
    per_token = expert_ids.shape[1]
    experts = PEERS * Z
    capacity = min(tok_rows, tok_rows * per_token // experts + tok_rows // 64)
    width = shared_out.shape[0]
    group = Z * capacity
    each = group + width
    line_rows = Z * tok_rows
    w_in, w_out = w_in[0], w_out[0]
    z_own, dp_own = lax.axis_index("z"), lax.axis_index("dp")

    def exchange(rows):
        rows = rows.reshape(PEERS, each, features)
        return lax.all_to_all(rows, ("x", "c"), split_axis=0, concat_axis=0, tiled=True)

    def placed(units):
        return jnp.pad(units, ((0, 0), (group, 0), (0, 0)))

    def gather_line(block):
        line = []

        def put(got, k, row):
            if not line:
                line.append(after(jnp.zeros((line_rows, features), BF16), got))
            at = ((z_own + k) % Z) * tok_rows
            line[0] = lax.dynamic_update_slice(line[0], got, (at + row, 0))

        rounds = gather_ring(block, "z", Z, put)
        return line[0], rounds

    def scatter_line(parts):
        def block(k, earlier=None):
            return lax.dynamic_slice_in_dim(parts, ((z_own + k) % Z) * tok_rows, tok_rows, axis=0)

        total, sent = scatter_ring(block, "z", Z)
        return total.astype(BF16), sent

    order = np.arange(experts).reshape(X, Z, C).transpose(1, 0, 2).reshape(experts)
    named = expert_ids.T[None] == jnp.asarray(order, jnp.int32)[:, None, None]
    chosen = jnp.sum(jnp.where(named, gate_units.T[None], 0), axis=1)
    dense = (chosen.astype(F32) / 256.0).astype(BF16).reshape(Z, PEERS, tok_rows)

    line_tokens, rounds = gather_line(tokens)
    dense = after(dense, *rounds[0])
    dense = lax.all_to_all(dense, "z", split_axis=0, concat_axis=0, tiled=True)
    dense = after(dense, *rounds[1])
    routed = dense > 0
    before = (
        lax.broadcasted_iota(jnp.int32, (tok_rows, tok_rows), 0)
        < lax.broadcasted_iota(jnp.int32, (tok_rows, tok_rows), 1)
    ).astype(BF16)
    rank = contract(routed.astype(BF16).reshape(experts, tok_rows), before, 1, 0)
    rank = rank.reshape(Z, PEERS, tok_rows).astype(jnp.int32)
    first = (jnp.arange(Z, dtype=jnp.int32) * capacity)[:, None, None]
    slot = jnp.where(routed, rank + first, -1)
    slot = slot.transpose(1, 0, 2).reshape(PEERS, 1, line_rows)
    gates = dense.transpose(1, 0, 2).reshape(PEERS, 1, line_rows)
    taken = lax.broadcasted_iota(jnp.int32, (PEERS, each, line_rows), 1) == slot
    pick = taken.astype(BF16).reshape(PEERS * each, line_rows)
    weigh = jnp.where(taken, gates, jnp.zeros((), BF16)).reshape(PEERS * each, line_rows)

    line_cotangent, rounds = gather_line(after(cotangent, *rounds[2]))

    def leaving(select, line, units):
        rows = contract(select, line, 1, 0).reshape(PEERS, each, features)
        return (rows + placed(units[None]).astype(F32)).astype(BF16)

    arrived = exchange(leaving(pick, line_tokens, shared_in.T))
    leaving_back = leaving(weigh, line_cotangent, shared_out)
    grad_rows = exchange(leaving_back)

    share = PEERS // DP * each
    units = PEERS // DP * width

    def part_of(rows, shared, weight, axis):
        rows = rows.reshape(PEERS * each, features)
        shared = shared.reshape(DP, PEERS // DP, width, line_rows)

        def block(k, earlier=None):
            at = (dp_own + k) % DP
            mine = rows if earlier is None else after(rows, earlier)
            mine = lax.dynamic_slice_in_dim(mine, at * share, share, axis=0)
            out = contract(mine, weight, 1, axis).astype(BF16).reshape(PEERS // DP, each, line_rows)
            ours = lax.dynamic_index_in_dim(shared, at, 0, keepdims=False)
            return lax.dynamic_update_slice(out, ours, (0, group, 0)).reshape(share, line_rows)

        return block

    def whole(block):
        everything = []

        def put(got, k, row):
            if not everything:
                everything.append(after(jnp.zeros((PEERS * each, line_rows), BF16), got))
            at = ((dp_own + k) % DP) * share + row
            everything[0] = lax.dynamic_update_slice(everything[0], got, (at, 0))

        gather_ring(block, "dp", DP, put)
        return everything[0]

    def shared_rows(rows):
        return rows.reshape(PEERS, each, -1)[:, group:]

    line_in = shared_rows(arrived).reshape(PEERS * width, features)
    shared_fwd = contract(line_in, line_tokens, 1, 1).astype(BF16)
    pre_act, sent = scatter_ring(part_of(arrived, shared_fwd, w_in, 0), "dp", DP)
    hidden_share, slope = together(jax.nn.silu(pre_act).astype(BF16), silu_slope(pre_act))
    hidden = whole(hidden_share)

    grad_rows = after(grad_rows, *sent[0])
    line_out = shared_rows(grad_rows).reshape(PEERS * width, features)
    shared_bwd = contract(line_out, line_cotangent, 1, 1).astype(BF16)
    hidden_grad, _ = scatter_ring(part_of(grad_rows, shared_bwd, w_out, 1), "dp", DP, hidden_share)

    routed_row = (jnp.arange(PEERS * each, dtype=jnp.int32) % each < group)[:, None]

    def returning(rows, weight, axis, line, *earlier):
        out = contract(rows, weight, 1, axis).astype(BF16).reshape(PEERS, each, features)
        units = shared_rows(rows).reshape(PEERS * width, line_rows)
        units = after(units, *earlier) if earlier else units
        terms = contract(units, line, 1, 0).astype(BF16).reshape(PEERS, width, features)
        return lax.dynamic_update_slice(out, terms, (0, group, 0)), units

    made, shared_hidden = returning(hidden, w_out, 0, line_cotangent)
    returned = exchange(made)
    pre_grad = whole((after(hidden_grad, made) * slope).astype(BF16))
    late_hidden = after(jnp.where(routed_row, hidden, 0), made)
    grad_w_out = contract(late_hidden, grad_rows.reshape(PEERS * each, features), 0, 0)
    back, shared_pgrad = returning(pre_grad, w_in, 1, line_tokens, returned)
    sent_back = exchange(back)
    returned = after(returned, back)
    mixed_part = contract(weigh, returned.reshape(PEERS * each, features), 0, 0)
    mixed_part = mixed_part + contract(shared_hidden, line_out, 0, 0)
    mixed_out, sent = scatter_line(mixed_part.astype(BF16))
    late_grad = after(jnp.where(routed_row, pre_grad, 0), back)
    grad_w_in = contract(arrived.reshape(PEERS * each, features), late_grad, 0, 0)
    sent_back, *_ = together(sent_back, grad_w_in, grad_w_out, *sent[1])
    grad_part = contract(pick, sent_back.reshape(PEERS * each, features), 0, 0)
    grad_part = grad_part + contract(shared_pgrad, line_in, 0, 0)
    input_grad, _ = scatter_line(grad_part.astype(BF16))
    grad_shared_in = jnp.sum(shared_rows(sent_back).astype(F32), axis=0)
    grad_shared_out = jnp.sum(shared_rows(returned).astype(F32), axis=0)
    return (
        mixed_out,
        input_grad,
        grad_w_in.astype(BF16)[None],
        grad_w_out.astype(BF16)[None],
        grad_shared_in.astype(BF16).T,
        grad_shared_out.astype(BF16),
    )


def solution(mesh):
    grid = Mesh(mesh.devices.reshape(X, Z, C, DP), ("x", "z", "c", "dp"))
    expert = ("x", "z", "c")
    return jax.shard_map(
        local,
        mesh=grid,
        in_specs=(
            P(expert, "dp"),
            P(expert, "dp"),
            P(expert, None),
            P(expert, None),
            P(expert, "dp", None),
            P(expert, None, "dp"),
            P("dp", expert),
            P(expert, "dp"),
        ),
        out_specs=(
            P(expert, "dp"),
            P(expert, "dp"),
            P(expert, "dp", None),
            P(expert, None, "dp"),
            P("dp", expert),
            P(expert, "dp"),
        ),
        check_vma=False,
    )
```

```python
import jax
import jax.numpy as jnp
import numpy as np
from jax import lax
from jax.sharding import Mesh, PartitionSpec as P

X, Z, C, DP = 4, 8, 2, 4
PEERS = X * C
BF16, F32 = jnp.bfloat16, jnp.float32


def silu_slope(inputs):
    logistic = jax.nn.sigmoid(inputs)
    return logistic * (1.0 + inputs * (1.0 - logistic))


def contract(first_op, second_op, first_axis, second_axis):
    return lax.dot_general(
        first_op,
        second_op,
        (((first_axis,), (second_axis,)), ((), ())),
        preferred_element_type=F32,
    )


def shifted(value, axis, size, step):
    return lax.ppermute(value, axis, [(i, (i + step) % size) for i in range(size)])


def together(*values):
    return lax.optimization_barrier(values)


def after(value, *earlier):
    return together(value, *earlier)[0]


def gather_ring(block, axis, size, put):
    half = block.shape[0] // 2
    put(block, 0, 0)
    back = ahead = block
    rounds = []
    for k in range(1, size // 2):
        back, ahead = together(shifted(back, axis, size, 1), shifted(ahead, axis, size, -1))
        rounds.append((back, ahead))
        put(back, size - k, 0)
        put(ahead, k, 0)
    put(shifted(back[:half], axis, size, 1), size // 2, 0)
    put(shifted(ahead[half:], axis, size, -1), size // 2, half)
    return rounds


def add(first, second):
    return (first.astype(F32) + second.astype(F32)).astype(BF16)


def scatter_ring(block, axis, size, gate=None):
    mid = size // 2
    far = block(mid)
    if gate is not None:
        far = after(far, gate)
    half = far.shape[0] // 2
    low = shifted(far[:half], axis, size, 1)
    high = shifted(far[half:], axis, size, -1)
    up, down = block(mid - 1, far), block(mid + 1, far)
    up = jnp.concatenate([add(up[:half], low), up[half:]], axis=0)
    down = jnp.concatenate([down[:half], add(down[half:], high)], axis=0)
    sent = []
    for k in range(mid - 1, 0, -1):
        up, down = together(up, down)
        sent.append((up, down))
        up = shifted(up, axis, size, 1)
        down = shifted(down, axis, size, -1)
        if k > 1:
            up = add(block(k - 1), up)
            down = add(block(size - k + 1), down)
    return block(0).astype(F32) + up.astype(F32) + down.astype(F32), sent


def local(tokens, cotangent, expert_ids, gate_units, w_in, w_out, shared_in, shared_out):
    tok_rows, features = tokens.shape
    per_token = expert_ids.shape[1]
    experts = PEERS * Z
    capacity = min(tok_rows, tok_rows * per_token // experts + tok_rows // 64)
    width = shared_out.shape[0]
    group = Z * capacity
    each = group + width
    line_rows = Z * tok_rows
    w_in, w_out = w_in[0], w_out[0]
    z_own, dp_own = lax.axis_index("z"), lax.axis_index("dp")

    def exchange(rows):
        rows = rows.reshape(PEERS, each, features)
        return lax.all_to_all(rows, ("x", "c"), split_axis=0, concat_axis=0, tiled=True)

    def placed(units):
        return jnp.pad(units, ((0, 0), (group, 0), (0, 0)))

    def gather_line(block):
        line = [jnp.zeros((line_rows, features), BF16)]

        def put(got, k, row):
            at = ((z_own + k) % Z) * tok_rows
            line[0] = lax.dynamic_update_slice(line[0], got, (at + row, 0))

        rounds = gather_ring(block, "z", Z, put)
        return line[0], rounds

    def scatter_line(parts):
        def block(k, earlier=None):
            return lax.dynamic_slice_in_dim(parts, ((z_own + k) % Z) * tok_rows, tok_rows, axis=0)

        total, sent = scatter_ring(block, "z", Z)
        return total.astype(BF16), sent

    order = np.arange(experts).reshape(X, Z, C).transpose(1, 0, 2).reshape(experts)
    named = expert_ids.T[None] == jnp.asarray(order, jnp.int32)[:, None, None]
    chosen = jnp.sum(jnp.where(named, gate_units.T[None], 0), axis=1)
    dense = (chosen.astype(F32) / 256.0).astype(BF16).reshape(Z, PEERS, tok_rows)

    line_tokens, rounds = gather_line(tokens)
    dense = after(dense, *rounds[0])
    dense = lax.all_to_all(dense, "z", split_axis=0, concat_axis=0, tiled=True)
    dense = after(dense, *rounds[1])
    routed = dense > 0
    before = (
        lax.broadcasted_iota(jnp.int32, (tok_rows, tok_rows), 0)
        < lax.broadcasted_iota(jnp.int32, (tok_rows, tok_rows), 1)
    ).astype(BF16)
    rank = contract(routed.astype(BF16).reshape(experts, tok_rows), before, 1, 0)
    rank = rank.reshape(Z, PEERS, tok_rows).astype(jnp.int32)
    first = (jnp.arange(Z, dtype=jnp.int32) * capacity)[:, None, None]
    slot = jnp.where(routed, rank + first, -1)
    slot = slot.transpose(1, 0, 2).reshape(PEERS, 1, line_rows)
    gates = dense.transpose(1, 0, 2).reshape(PEERS, 1, line_rows)
    taken = lax.broadcasted_iota(jnp.int32, (PEERS, each, line_rows), 1) == slot
    pick = taken.astype(BF16).reshape(PEERS * each, line_rows)
    weigh = jnp.where(taken, gates, jnp.zeros((), BF16)).reshape(PEERS * each, line_rows)

    line_cotangent, rounds = gather_line(after(cotangent, *rounds[2]))

    def leaving(select, line, units):
        rows = contract(select, line, 1, 0).reshape(PEERS, each, features)
        return (rows + placed(units[None]).astype(F32)).astype(BF16)

    arrived = exchange(leaving(pick, line_tokens, shared_in.T))
    leaving_back = leaving(weigh, line_cotangent, shared_out)
    grad_rows = exchange(leaving_back)

    share = PEERS // DP * each
    units = PEERS // DP * width

    def part_of(rows, shared, weight, axis):
        rows = rows.reshape(PEERS * each, features)
        shared = shared.reshape(DP, PEERS // DP, width, line_rows)

        def block(k, earlier=None):
            at = (dp_own + k) % DP
            mine = rows if earlier is None else after(rows, earlier)
            mine = lax.dynamic_slice_in_dim(mine, at * share, share, axis=0)
            out = contract(mine, weight, 1, axis).astype(BF16).reshape(PEERS // DP, each, line_rows)
            ours = lax.dynamic_index_in_dim(shared, at, 0, keepdims=False)
            return lax.dynamic_update_slice(out, ours, (0, group, 0)).reshape(share, line_rows)

        return block

    def whole(block):
        everything = [jnp.zeros((PEERS * each, line_rows), BF16)]

        def put(got, k, row):
            at = ((dp_own + k) % DP) * share + row
            everything[0] = lax.dynamic_update_slice(everything[0], got, (at, 0))

        gather_ring(block, "dp", DP, put)
        return everything[0]

    def shared_rows(rows):
        return rows.reshape(PEERS, each, -1)[:, group:]

    line_in = shared_rows(arrived).reshape(PEERS * width, features)
    shared_fwd = contract(line_in, line_tokens, 1, 1).astype(BF16)
    pre_act, sent = scatter_ring(part_of(arrived, shared_fwd, w_in, 0), "dp", DP)
    hidden_share, slope = together(jax.nn.silu(pre_act).astype(BF16), silu_slope(pre_act))
    hidden = whole(hidden_share)

    grad_rows = after(grad_rows, *sent[0])
    line_out = shared_rows(grad_rows).reshape(PEERS * width, features)
    shared_bwd = contract(line_out, line_cotangent, 1, 1).astype(BF16)
    hidden_grad, _ = scatter_ring(part_of(grad_rows, shared_bwd, w_out, 1), "dp", DP, hidden_share)

    routed_row = (jnp.arange(PEERS * each, dtype=jnp.int32) % each < group)[:, None]

    def returning(rows, weight, axis, line, *earlier):
        out = contract(rows, weight, 1, axis).astype(BF16).reshape(PEERS, each, features)
        units = shared_rows(rows).reshape(PEERS * width, line_rows)
        units = after(units, *earlier) if earlier else units
        terms = contract(units, line, 1, 0).astype(BF16).reshape(PEERS, width, features)
        return lax.dynamic_update_slice(out, terms, (0, group, 0)), units

    made, shared_hidden = returning(hidden, w_out, 0, line_cotangent)
    returned = exchange(made)
    pre_grad = whole((after(hidden_grad, made) * slope).astype(BF16))
    late_hidden = after(jnp.where(routed_row, hidden, 0), made)
    grad_w_out = contract(late_hidden, grad_rows.reshape(PEERS * each, features), 0, 0)
    back, shared_pgrad = returning(pre_grad, w_in, 1, line_tokens, returned)
    sent_back = exchange(back)
    returned = after(returned, back)
    mixed_part = contract(weigh, returned.reshape(PEERS * each, features), 0, 0)
    mixed_part = mixed_part + contract(shared_hidden, line_out, 0, 0)
    mixed_out, sent = scatter_line(mixed_part.astype(BF16))
    late_grad = after(jnp.where(routed_row, pre_grad, 0), back)
    grad_w_in = contract(arrived.reshape(PEERS * each, features), late_grad, 0, 0)
    grad_shared_out = jnp.sum(shared_rows(returned).astype(F32), axis=0)
    sent_back, *_ = together(sent_back, grad_w_in, grad_w_out, grad_shared_out, *sent[1])
    grad_part = contract(pick, sent_back.reshape(PEERS * each, features), 0, 0)
    grad_part = grad_part + contract(shared_pgrad, line_in, 0, 0)
    input_grad, _ = scatter_line(grad_part.astype(BF16))
    grad_shared_in = jnp.sum(shared_rows(sent_back).astype(F32), axis=0)
    return (
        mixed_out,
        input_grad,
        grad_w_in.astype(BF16)[None],
        grad_w_out.astype(BF16)[None],
        grad_shared_in.astype(BF16).T,
        grad_shared_out.astype(BF16),
    )


def solution(mesh):
    grid = Mesh(mesh.devices.reshape(X, Z, C, DP), ("x", "z", "c", "dp"))
    expert = ("x", "z", "c")
    return jax.shard_map(
        local,
        mesh=grid,
        in_specs=(
            P(expert, "dp"),
            P(expert, "dp"),
            P(expert, None),
            P(expert, None),
            P(expert, "dp", None),
            P(expert, None, "dp"),
            P("dp", expert),
            P(expert, "dp"),
        ),
        out_specs=(
            P(expert, "dp"),
            P(expert, "dp"),
            P(expert, "dp", None),
            P(expert, None, "dp"),
            P("dp", expert),
            P(expert, "dp"),
        ),
        check_vma=False,
    )
```

```python
import jax
import jax.numpy as jnp
import numpy as np
from jax import lax
from jax.sharding import Mesh, PartitionSpec as P

X, Z, C, DP = 4, 8, 2, 4
PEERS = X * C
BF16, F32 = jnp.bfloat16, jnp.float32


def silu_slope(inputs):
    logistic = jax.nn.sigmoid(inputs)
    return logistic * (1.0 + inputs * (1.0 - logistic))


def contract(first_op, second_op, first_axis, second_axis):
    return lax.dot_general(
        first_op,
        second_op,
        (((first_axis,), (second_axis,)), ((), ())),
        preferred_element_type=F32,
    )


def shifted(value, axis, size, step):
    return lax.ppermute(value, axis, [(i, (i + step) % size) for i in range(size)])


def together(*values):
    return lax.optimization_barrier(values)


def after(value, *earlier):
    return together(value, *earlier)[0]


def gather_ring(block, axis, size, put):
    half = block.shape[0] // 2
    put(block, 0, 0)
    back = ahead = block
    rounds = []
    for k in range(1, size // 2):
        back, ahead = together(shifted(back, axis, size, 1), shifted(ahead, axis, size, -1))
        rounds.append((back, ahead))
        put(back, size - k, 0)
        put(ahead, k, 0)
    put(shifted(back[:half], axis, size, 1), size // 2, 0)
    put(shifted(ahead[half:], axis, size, -1), size // 2, half)
    return rounds


def add(first, second):
    return (first.astype(F32) + second.astype(F32)).astype(BF16)


def scatter_ring(block, axis, size, gate=None):
    mid = size // 2
    far = block(mid)
    if gate is not None:
        far = after(far, gate)
    half = far.shape[0] // 2
    low = shifted(far[:half], axis, size, 1)
    high = shifted(far[half:], axis, size, -1)
    up, down = block(mid - 1, far), block(mid + 1, far)
    up = jnp.concatenate([add(up[:half], low), up[half:]], axis=0)
    down = jnp.concatenate([down[:half], add(down[half:], high)], axis=0)
    sent = []
    for k in range(mid - 1, 0, -1):
        up, down = together(up, down)
        sent.append((up, down))
        up = shifted(up, axis, size, 1)
        down = shifted(down, axis, size, -1)
        if k > 1:
            up = add(block(k - 1), up)
            down = add(block(size - k + 1), down)
    return block(0).astype(F32) + up.astype(F32) + down.astype(F32), sent


def local(tokens, cotangent, expert_ids, gate_units, w_in, w_out, shared_in, shared_out):
    tok_rows, features = tokens.shape
    per_token = expert_ids.shape[1]
    experts = PEERS * Z
    capacity = min(tok_rows, tok_rows * per_token // experts + tok_rows // 64)
    width = shared_out.shape[0]
    group = Z * capacity
    each = group + width
    line_rows = Z * tok_rows
    w_in, w_out = w_in[0], w_out[0]
    z_own, dp_own = lax.axis_index("z"), lax.axis_index("dp")

    def exchange(rows):
        rows = rows.reshape(PEERS, each, features)
        return lax.all_to_all(rows, ("x", "c"), split_axis=0, concat_axis=0, tiled=True)

    def placed(units):
        return jnp.pad(units, ((0, 0), (group, 0), (0, 0)))

    def gather_line(block):
        line = [jnp.zeros((line_rows, features), BF16)]

        def put(got, k, row):
            at = ((z_own + k) % Z) * tok_rows
            line[0] = lax.dynamic_update_slice(line[0], got, (at + row, 0))

        rounds = gather_ring(block, "z", Z, put)
        return line[0], rounds

    def scatter_line(parts):
        def block(k, earlier=None):
            return lax.dynamic_slice_in_dim(parts, ((z_own + k) % Z) * tok_rows, tok_rows, axis=0)

        total, sent = scatter_ring(block, "z", Z)
        return total.astype(BF16), sent

    order = np.arange(experts).reshape(X, Z, C).transpose(1, 0, 2).reshape(experts)
    named = expert_ids.T[None] == jnp.asarray(order, jnp.int32)[:, None, None]
    chosen = jnp.sum(jnp.where(named, gate_units.T[None], 0), axis=1)
    dense = (chosen.astype(F32) / 256.0).astype(BF16).reshape(Z, PEERS, tok_rows)

    line_tokens, rounds = gather_line(tokens)
    dense = after(dense, *rounds[0])
    dense = lax.all_to_all(dense, "z", split_axis=0, concat_axis=0, tiled=True)
    dense = after(dense, *rounds[1])
    routed = dense > 0
    before = (
        lax.broadcasted_iota(jnp.int32, (tok_rows, tok_rows), 0)
        < lax.broadcasted_iota(jnp.int32, (tok_rows, tok_rows), 1)
    ).astype(BF16)
    rank = contract(routed.astype(BF16).reshape(experts, tok_rows), before, 1, 0)
    rank = rank.reshape(Z, PEERS, tok_rows).astype(jnp.int32)
    first = (jnp.arange(Z, dtype=jnp.int32) * capacity)[:, None, None]
    slot = jnp.where(routed, rank + first, -1)
    slot = slot.transpose(1, 0, 2).reshape(PEERS, 1, line_rows)
    gates = dense.transpose(1, 0, 2).reshape(PEERS, 1, line_rows)
    taken = lax.broadcasted_iota(jnp.int32, (PEERS, each, line_rows), 1) == slot
    pick = taken.astype(BF16).reshape(PEERS * each, line_rows)
    weigh = jnp.where(taken, gates, jnp.zeros((), BF16)).reshape(PEERS * each, line_rows)

    line_cotangent, rounds = gather_line(after(cotangent, *rounds[2]))

    def leaving(select, line, units):
        rows = contract(select, line, 1, 0).reshape(PEERS, each, features)
        return (rows + placed(units[None]).astype(F32)).astype(BF16)

    arrived = exchange(leaving(pick, line_tokens, shared_in.T))
    leaving_back = leaving(weigh, line_cotangent, shared_out)
    grad_rows = exchange(leaving_back)

    share = PEERS // DP * each
    units = PEERS // DP * width

    def part_of(rows, shared, weight, axis):
        rows = rows.reshape(PEERS * each, features)
        shared = shared.reshape(DP, PEERS // DP, width, line_rows)

        def block(k, earlier=None):
            at = (dp_own + k) % DP
            mine = rows if earlier is None else after(rows, earlier)
            mine = lax.dynamic_slice_in_dim(mine, at * share, share, axis=0)
            out = contract(mine, weight, 1, axis).astype(BF16).reshape(PEERS // DP, each, line_rows)
            ours = lax.dynamic_index_in_dim(shared, at, 0, keepdims=False)
            return lax.dynamic_update_slice(out, ours, (0, group, 0)).reshape(share, line_rows)

        return block

    def whole(block):
        everything = [jnp.zeros((PEERS * each, line_rows), BF16)]

        def put(got, k, row):
            at = ((dp_own + k) % DP) * share + row
            everything[0] = lax.dynamic_update_slice(everything[0], got, (at, 0))

        rounds = gather_ring(block, "dp", DP, put)
        return everything[0], rounds[0][0]

    def shared_rows(rows):
        return rows.reshape(PEERS, each, -1)[:, group:]

    line_in = shared_rows(arrived).reshape(PEERS * width, features)
    shared_fwd = contract(line_in, line_tokens, 1, 1).astype(BF16)
    pre_act, sent = scatter_ring(part_of(arrived, shared_fwd, w_in, 0), "dp", DP)
    hidden_share, slope = together(jax.nn.silu(pre_act).astype(BF16), silu_slope(pre_act))
    hidden, passed = whole(hidden_share)

    grad_rows = after(grad_rows, *sent[0])
    line_out = shared_rows(grad_rows).reshape(PEERS * width, features)
    shared_bwd = contract(line_out, line_cotangent, 1, 1).astype(BF16)
    hidden_grad, _ = scatter_ring(part_of(grad_rows, shared_bwd, w_out, 1), "dp", DP, passed)

    routed_row = (jnp.arange(PEERS * each, dtype=jnp.int32) % each < group)[:, None]

    def returning(rows, weight, axis, line, *earlier):
        out = contract(rows, weight, 1, axis).astype(BF16).reshape(PEERS, each, features)
        units = shared_rows(rows).reshape(PEERS * width, line_rows)
        units = after(units, *earlier) if earlier else units
        terms = contract(units, line, 1, 0).astype(BF16).reshape(PEERS, width, features)
        return lax.dynamic_update_slice(out, terms, (0, group, 0)), units

    made, shared_hidden = returning(hidden, w_out, 0, line_cotangent)
    returned = exchange(made)
    pre_grad, _ = whole((after(hidden_grad, made) * slope).astype(BF16))
    late_hidden = after(jnp.where(routed_row, hidden, 0), made)
    grad_w_out = contract(late_hidden, grad_rows.reshape(PEERS * each, features), 0, 0)
    back, shared_pgrad = returning(pre_grad, w_in, 1, line_tokens, returned)
    sent_back = exchange(back)
    returned = after(returned, back)
    mixed_part = contract(weigh, returned.reshape(PEERS * each, features), 0, 0)
    mixed_part = mixed_part + contract(shared_hidden, line_out, 0, 0)
    mixed_out, sent = scatter_line(mixed_part.astype(BF16))
    late_grad = after(jnp.where(routed_row, pre_grad, 0), back)
    grad_w_in = contract(arrived.reshape(PEERS * each, features), late_grad, 0, 0)
    grad_shared_out = jnp.sum(shared_rows(returned).astype(F32), axis=0)
    sent_back, *_ = together(sent_back, grad_w_in, grad_w_out, grad_shared_out, *sent[1])
    grad_part = contract(pick, sent_back.reshape(PEERS * each, features), 0, 0)
    grad_part = grad_part + contract(shared_pgrad, line_in, 0, 0)
    input_grad, _ = scatter_line(grad_part.astype(BF16))
    grad_shared_in = jnp.sum(shared_rows(sent_back).astype(F32), axis=0)
    return (
        mixed_out,
        input_grad,
        grad_w_in.astype(BF16)[None],
        grad_w_out.astype(BF16)[None],
        grad_shared_in.astype(BF16).T,
        grad_shared_out.astype(BF16),
    )


def solution(mesh):
    grid = Mesh(mesh.devices.reshape(X, Z, C, DP), ("x", "z", "c", "dp"))
    expert = ("x", "z", "c")
    return jax.shard_map(
        local,
        mesh=grid,
        in_specs=(
            P(expert, "dp"),
            P(expert, "dp"),
            P(expert, None),
            P(expert, None),
            P(expert, "dp", None),
            P(expert, None, "dp"),
            P("dp", expert),
            P(expert, "dp"),
        ),
        out_specs=(
            P(expert, "dp"),
            P(expert, "dp"),
            P(expert, "dp", None),
            P(expert, None, "dp"),
            P("dp", expert),
            P(expert, "dp"),
        ),
        check_vma=False,
    )
```
